32 devices in a mesh: lists: 4 (over x, core), score: 8 (over z, y).
Axes of the slice: x: 2, y: 2, z: 4, core: 2. Of those that a mesh axis runs over, the one named last changes fastest.
Arguments:
- queries: bfloat16 [256, 32, 128], P('score', 'lists'), may hold values from -0.59765625 to 0.59765625
- centroids: bfloat16 [32768, 128], P('lists'), may hold values from -3 to 3
- codes: bfloat16 [1024, 128, 128], P(('lists', 'score')), may hold values from -6 to 6
- scales: float32 [1024, 128], P(('lists', 'score')), may hold values from 0.1 to 1
- centroid_ids: int32 [1024, 128], P(('lists', 'score')), may hold values from 0 to 8191
- lengths: int32 [1024], P(('lists', 'score')), may hold values from 1 to 128
- owners: int32 [4, 256, 8], P('lists', 'score'), may hold values from 0 to 31, all different within a row; in each aligned block of 32 rows (0 to 31, 32 to 63, ..., all dimensions but the last counted through in order) at most 16 rows name the same one
- slots: int32 [4, 256, 8], P('lists', 'score'), may hold values from 0 to 31
Outputs:
- scores: float32 [4, 256, 8], P('lists', 'score')
- relevance: float32 [256, 32768], P('score', 'lists')
The draws below stay inside these ranges and needn't reach their ends.
Inputs may be any that keep to these rules, and one draw needn't show every extreme that they name: Within the 32 rows of one device (aligned blocks of 32 rows, the first two dimensions taken together in order) no owner is named more than 16 times; each row names 8 different owners. Owner d holds blocks d * 32 to d * 32 + 31. `centroid_ids`: A row among the 8192 centroids of the block's lists shard.
All inputs are finite; a program needn't handle non-finite values.
Results may differ from the reference program's by a relative error of at most 0.00034.
Values may be sent and summed in bfloat16 or wider, within the bound.
A program may use at most 128 MiB of HBM per device.

```python
import math
import jax
import jax.numpy as jnp
import numpy as np
from jax import lax

DIM = 128
QT = 32
PT = 128
CENT_DEV = 8192
Q_DEV = 32
CSL = 8
BLK_DEV = 32
NCENT = 32768
Q = 256
BLOCKS = 1024
SHARD_BLOCKS = 256
CAP = 16
N_LISTS = 4
DEVICES = 32


def place_ends(array, key, low, largest):
    index_at = [jax.random.randint(jax.random.fold_in(key, axis), (), 0, length) for axis, length in enumerate(array.shape)]
    main_axis = array.shape.index(max(array.shape))
    beside = index_at[:main_axis] + [(index_at[main_axis] + 1) % array.shape[main_axis]] + index_at[main_axis + 1:]
    return array.at[tuple(index_at)].set(low).at[tuple(beside)].set(largest)


def block_scale(rng, extent, pieces, least, largest):
    def one(dim, parts):
        steps = jax.random.uniform(jax.random.fold_in(jax.random.fold_in(rng, 6), dim), (parts,), jnp.float32, least / len(pieces), largest / len(pieces))
        return jnp.repeat(jnp.exp(steps), extent[dim] // parts).reshape((-1,) + (1,) * (len(extent) - dim - 1))

    loudness = one(*pieces[0])
    for cut in pieces[1:]:
        loudness = loudness * one(*cut)
    return loudness


def routed_block(rng, own, number, rows, count, top, limit, slope):
    order = jax.random.permutation(rng, count)
    packed, usual = portions_of(count, rows * top, limit, slope, True), portions_of(count, rows * top, limit, slope, False)
    places = jnp.arange(count)

    def named(sizes, offset_by):
        used = int((sizes > 0).sum())
        fixed = max(1, used // 4)
        moved = fixed + (places - fixed + offset_by * (used - fixed)) % max(1, count - fixed)
        return jnp.zeros((count,), jnp.int32).at[order[jnp.where(places < fixed, places, moved)]].set(jnp.asarray(sizes, jnp.int32))

    sizes = jnp.where(number % 4 == 0, named(packed, number // 4), named(usual, number - number // 4 - 1))
    mixed = jax.random.permutation(jax.random.fold_in(own, 3), count)
    giver, receiver = mixed[0:count // 2 * 2:2], mixed[1:count // 2 * 2:2]
    margin = jnp.minimum(sizes[giver] - 1, limit - sizes[receiver]) // 2
    margin = jnp.where((giver == order[0]) | (receiver == order[0]) | (sizes[receiver] == 0), 0, jnp.maximum(margin, 0))
    moved = jax.random.randint(jax.random.fold_in(own, 4), (count // 2,), 0, 1 << 20) % (margin + 1)
    sizes = sizes.at[giver].add(-moved).at[receiver].add(moved)
    items = jnp.searchsorted(jnp.cumsum(sizes), jnp.arange(rows * top), side="right").astype(jnp.int32)
    table = items.reshape(top, rows).T
    table = table[jax.random.permutation(jax.random.fold_in(own, 1), rows)]
    offset_by = jax.random.randint(jax.random.fold_in(own, 2), (rows, 1), 0, top)
    return jnp.take_along_axis(table, (jnp.arange(top)[None, :] + offset_by) % top, axis=1)


def portions_of(count, total, limit, lean, full):
    loads = [(1 << 20) // math.isqrt(standing ** lean) + 1 for standing in range(1, count + 1)]
    largest = limit if full else min(limit, max(-(-total // count), total * loads[0] // sum(loads)))
    least = 1 if total - largest >= count - 1 else 0
    given, rest = [largest] + [least] * (count - 1), total - largest - least * (count - 1)
    while rest > 0:
        free = [i for i in range(1, count) if given[i] < largest] or [i for i in range(1, count) if given[i] < limit]
        whole, left = sum([loads[i] for i in free]), rest
        for i in free:
            extra = min(limit - given[i], max(1, left * loads[i] // whole), rest)
            given[i] = given[i] + extra
            rest = rest - extra
    return np.array(given)


def centred(rng, shape, deviation, bound, pieces=(), kind=jnp.bfloat16):
    gain = block_scale(rng, shape, pieces, -0.22, 0.18) if pieces else 1.0
    result = jax.random.normal(rng, shape, jnp.float32) * deviation * gain
    return jnp.minimum(jnp.maximum(result, -bound), bound).astype(kind)


def setup_inputs(seed: int = 0) -> dict:
    key_list = jax.random.split(jax.random.key(seed), 9)
    queries = centred(key_list[0], (Q, QT, DIM), 0.1, 0.59765625, ((0, 8), (1, 4)))
    centroids = centred(key_list[1], (NCENT, DIM), 0.5, 3.0, ((0, 4),))
    codes = centred(key_list[2], (BLOCKS, PT, DIM), 1.0, 6.0, ((0, 32),))
    scales = jnp.clip(jnp.exp(math.log(1.0) - 2.3025851 * jax.random.uniform(key_list[3], (BLOCKS, PT), jnp.float32) ** block_scale(key_list[3], (BLOCKS, PT), ((0, 32),), -0.2, 0.2)), 0.1, 1.0)
    centroid_ids = place_ends(jax.random.randint(key_list[4], (BLOCKS, PT), 0, CENT_DEV), jax.random.fold_in(key_list[4], 1), 0, CENT_DEV - 1).astype(jnp.int32)
    lengths = place_ends(jax.random.randint(key_list[5], (BLOCKS,), 1, PT + 1), jax.random.fold_in(key_list[5], 1), 1, PT).astype(jnp.int32)
    owners_keys = jax.random.split(jax.random.fold_in(key_list[6], 1), N_LISTS * Q // Q_DEV)
    owners_turns = jax.random.permutation(jax.random.fold_in(key_list[6], 3), N_LISTS * Q // Q_DEV)
    owners = jax.vmap(lambda own, number: routed_block(jax.random.fold_in(key_list[6], 2), own, number, Q_DEV, DEVICES, CSL, CAP, 2))(owners_keys, owners_turns).reshape((N_LISTS, Q, CSL))
    slots = place_ends(jax.random.randint(key_list[7], (N_LISTS, Q, CSL), 0, BLK_DEV), jax.random.fold_in(key_list[7], 1), 0, BLK_DEV - 1).astype(jnp.int32)
    return dict(queries=queries, centroids=centroids, codes=codes, scales=scales, centroid_ids=centroid_ids, lengths=lengths, owners=owners, slots=slots)


def rebuild(codes, scales, centroid_ids, centroids, wanted):
    shard = wanted // SHARD_BLOCKS
    rows_index = shard[..., None] * CENT_DEV + centroid_ids[wanted]
    base = centroids[rows_index].astype(jnp.float32)
    vectors = base + scales[wanted][..., None] * codes[wanted].astype(jnp.float32)
    return vectors.astype(jnp.bfloat16)


def reference(queries, centroids, codes, scales, centroid_ids, lengths, owners, slots):
    query_float = queries.astype(jnp.float32)
    block = (owners * BLK_DEV + slots).astype(jnp.int32)

    def score_shard(block_shard):
        vectors = rebuild(codes, scales, centroid_ids, centroids, block_shard)
        inner = jnp.einsum("qtd,qcpd->qctp", query_float, vectors.astype(jnp.float32))
        spots = jnp.arange(PT, dtype=jnp.int32)
        keep = spots[None, None, None, :] < lengths[block_shard][:, :, None, None]
        best = jnp.max(jnp.where(keep, inner, -1e30), axis=3)
        return jnp.sum(best, axis=2) / QT

    scores = lax.map(score_shard, block)
    group = math.gcd(NCENT, 4096)
    flat = queries.reshape(Q * QT, DIM)
    grouped = centroids.reshape(NCENT // group, group, DIM)

    def relate(block_rows):
        inner = lax.dot_general(flat, block_rows, (((1,), (1,)), ((), ())), preferred_element_type=jnp.float32)
        return jnp.max(inner.reshape(Q, QT, group), axis=1)

    related = lax.map(relate, grouped)
    relevance = jnp.transpose(related, (1, 0, 2)).reshape(Q, NCENT)
    return scores, relevance
```

```python
import functools

import jax
import jax.numpy as jnp
from jax import lax
from jax.experimental import pallas as pl
from jax.experimental.pallas import tpu as pltpu
from jax.sharding import PartitionSpec as P

PAIRS = 16
ROWS = 16
AXES = ("lists", "score")


def score_kernel(
    ids_ref, lens_ref, pickq_ref, picks_ref, cent_ref, codes_ref, scales_ref, q_ref, out_ref, wide, base, vecs
):
    held, slot_len, width = codes_ref.shape
    cent_rows = cent_ref.shape[0]
    step = 512

    @pl.loop(0, cent_rows // step)
    def _(i):
        rows = pl.ds(pl.multiple_of(i * step, step), step)
        wide[rows, :] = cent_ref[rows, :].astype(jnp.float32)

    @pl.loop(0, held)
    def _(b):
        @pl.loop(0, (lens_ref[b] + ROWS - 1) // ROWS)
        def _(r):
            first = pl.multiple_of(r * ROWS, ROWS)
            for j in range(ROWS):
                base[pl.ds(first + j, 1), :] = wide[pl.ds(ids_ref[b, first + j], 1), :]

        row = scales_ref[pl.ds(b, 1), :]
        spread = jnp.transpose(jnp.broadcast_to(row, (slot_len, slot_len)))
        if width != slot_len:
            spread = jnp.broadcast_to(spread[:, :1], (slot_len, width))
        vecs[b] = (base[...] + spread * codes_ref[b].astype(jnp.float32)).astype(jnp.bfloat16)

    lanes = lax.broadcasted_iota(jnp.int32, (1, slot_len), 1)

    @pl.loop(0, out_ref.shape[0])
    def _(i):
        acc = jnp.zeros((1, 128), jnp.float32)
        spots = lax.broadcasted_iota(jnp.int32, (1, 128), 1)
        for j in range(PAIRS):
            slot = picks_ref[i * PAIRS + j]
            inner = lax.dot_general(
                q_ref[pickq_ref[i * PAIRS + j]],
                vecs[slot],
                (((1,), (1,)), ((), ())),
                preferred_element_type=jnp.float32,
            )
            inner = jnp.where(lanes < lens_ref[slot], inner, -1e30)
            best = jnp.max(inner, axis=1, keepdims=True)
            total = jnp.sum(best, axis=0, keepdims=True)
            acc = jnp.where(spots == j, total, acc)
        out_ref[pl.ds(i, 1), :] = acc * (1.0 / q_ref.shape[1])


def score_pairs(ids, lens, pickq, picks, centroids, codes, scales, allq):
    held, slot_len, width = codes.shape
    smem = pl.BlockSpec(memory_space=pltpu.SMEM)
    vmem = pl.BlockSpec(memory_space=pltpu.VMEM)
    return pl.pallas_call(
        score_kernel,
        out_shape=jax.ShapeDtypeStruct((pickq.shape[0] // PAIRS, 128), jnp.float32),
        in_specs=[smem] * 4 + [vmem] * 4,
        out_specs=vmem,
        scratch_shapes=[
            pltpu.VMEM(centroids.shape, jnp.float32),
            pltpu.VMEM((slot_len, width), jnp.float32),
            pltpu.VMEM(codes.shape, jnp.bfloat16),
        ],
        compiler_params=pltpu.CompilerParams(vmem_limit_bytes=40 * 1024 * 1024),
    )(ids, lens, pickq, picks, centroids, codes, scales, allq)


def before(count):
    spots = jnp.arange(count, dtype=jnp.int32)
    return (spots[:, None] < spots[None, :]).astype(jnp.bfloat16)


def per_device(queries, centroids, codes, scales, centroid_ids, lengths, owners, slots):
    lists, score = lax.axis_size("lists"), lax.axis_size("score")
    devices = lists * score
    me = lax.axis_index("lists") * score + lax.axis_index("score")
    query_rows, per_query = owners.shape[1:]
    capacity = max(4, 2 * -(-query_rows * per_query // devices))
    held = codes.shape[0]

    mine = lax.all_gather(queries, "lists", axis=1, tiled=True)
    allq = lax.all_gather(mine, "score", axis=0, tiled=True)
    token_count, width = mine.shape[1:]
    asked = lax.all_gather(owners[0] * held + slots[0], AXES, axis=0)

    inner = lax.dot_general(
        mine.reshape(-1, width), centroids, (((1,), (1,)), ((), ())), preferred_element_type=jnp.float32
    )
    relevance = jnp.max(inner.reshape(query_rows, token_count, -1), axis=1)

    hit = asked // held == me
    named = jnp.any(hit, axis=2)
    slot = jnp.sum(jnp.where(hit, asked % held, 0), axis=2)
    place = jnp.dot(named.astype(jnp.bfloat16), before(query_rows), preferred_element_type=jnp.float32).astype(jnp.int32)
    take = named[:, None, :] & (place[:, None, :] == jnp.arange(capacity, dtype=jnp.int32)[None, :, None])
    group = jnp.arange(devices, dtype=jnp.int32) % score
    query = group[:, None] * query_rows + jnp.arange(query_rows, dtype=jnp.int32)[None, :]
    pickq = jnp.sum(jnp.where(take, query[:, None, :], 0), axis=2).reshape(-1)
    picks = jnp.sum(jnp.where(take, slot[:, None, :], 0), axis=2).reshape(-1)

    done = score_pairs(centroid_ids, lengths, pickq, picks, centroids, codes, scales, allq)
    done = done[:, :PAIRS].reshape(devices, capacity)
    full = jnp.sum(jnp.where(take, done[:, :, None], 0.0), axis=1)
    back = lax.all_to_all(full, AXES, split_axis=0, concat_axis=0, tiled=True)
    which = owners[0][:, :, None] == jnp.arange(devices, dtype=jnp.int32)
    scores = jnp.sum(jnp.where(which, jnp.transpose(back)[:, None, :], 0.0), axis=2)
    return (scores[None], relevance)


def solution(mesh):
    placed = (
        P("score", "lists", None),
        P("lists", None),
        P(("lists", "score"), None, None),
        P(("lists", "score"), None),
        P(("lists", "score"), None),
        P(("lists", "score")),
        P("lists", "score", None),
        P("lists", "score", None),
    )
    return jax.shard_map(
        per_device,
        mesh=mesh,
        in_specs=placed,
        out_specs=(P("lists", "score", None), P("score", "lists")),
        check_vma=False,
    )
```

```python
import functools
import itertools
import math

import jax
import jax.numpy as jnp
from jax import lax
from jax.experimental import pallas as pl
from jax.experimental.pallas import tpu as pltpu
from jax.sharding import PartitionSpec as P

PAIRS = 16
ROWS = 16
AXES = ("lists", "score")


def score_kernel(
    ids_ref, lens_ref, pickq_ref, picks_ref, cent_ref, codes_ref, scales_ref, q_ref, out_ref, wide, base, vecs
):
    held, slot_len, width = codes_ref.shape
    cent_rows = cent_ref.shape[0]
    step = 512

    @pl.loop(0, cent_rows // step)
    def _(i):
        rows = pl.ds(pl.multiple_of(i * step, step), step)
        wide[rows, :] = cent_ref[rows, :].astype(jnp.float32)

    @pl.loop(0, held)
    def _(b):
        @pl.loop(0, (lens_ref[b] + ROWS - 1) // ROWS)
        def _(r):
            first = pl.multiple_of(r * ROWS, ROWS)
            for j in range(ROWS):
                base[pl.ds(first + j, 1), :] = wide[pl.ds(ids_ref[b, first + j], 1), :]

        row = scales_ref[pl.ds(b, 1), :]
        spread = jnp.transpose(jnp.broadcast_to(row, (slot_len, slot_len)))
        if width != slot_len:
            spread = jnp.broadcast_to(spread[:, :1], (slot_len, width))
        vecs[b] = (base[...] + spread * codes_ref[b].astype(jnp.float32)).astype(jnp.bfloat16)

    lanes = lax.broadcasted_iota(jnp.int32, (1, slot_len), 1)

    @pl.loop(0, out_ref.shape[0])
    def _(i):
        acc = jnp.zeros((1, 128), jnp.float32)
        spots = lax.broadcasted_iota(jnp.int32, (1, 128), 1)
        for j in range(PAIRS):
            slot = picks_ref[i * PAIRS + j]
            inner = lax.dot_general(
                q_ref[pickq_ref[i * PAIRS + j]],
                vecs[slot],
                (((1,), (1,)), ((), ())),
                preferred_element_type=jnp.float32,
            )
            inner = jnp.where(lanes < lens_ref[slot], inner, -1e30)
            best = jnp.max(inner, axis=1, keepdims=True)
            total = jnp.sum(best, axis=0, keepdims=True)
            acc = jnp.where(spots == j, total, acc)
        out_ref[pl.ds(i, 1), :] = acc * (1.0 / q_ref.shape[1])


def score_pairs(ids, lens, pickq, picks, centroids, codes, scales, allq):
    held, slot_len, width = codes.shape
    smem = pl.BlockSpec(memory_space=pltpu.SMEM)
    vmem = pl.BlockSpec(memory_space=pltpu.VMEM)
    return pl.pallas_call(
        score_kernel,
        out_shape=jax.ShapeDtypeStruct((pickq.shape[0] // PAIRS, 128), jnp.float32),
        in_specs=[smem] * 4 + [vmem] * 4,
        out_specs=vmem,
        scratch_shapes=[
            pltpu.VMEM(centroids.shape, jnp.float32),
            pltpu.VMEM((slot_len, width), jnp.float32),
            pltpu.VMEM(codes.shape, jnp.bfloat16),
        ],
        compiler_params=pltpu.CompilerParams(vmem_limit_bytes=40 * 1024 * 1024),
    )(ids, lens, pickq, picks, centroids, codes, scales, allq)


MESH = pl.DeviceIdType.MESH


def split_sizes(lists, score):
    core = 2 if lists % 2 == 0 else 1
    inner = 2 if score <= 8 and score % 2 == 0 else math.gcd(score, 4)
    return (score // inner, inner, lists // core, core)


def spread_kernel(sizes, q_ref, asked_ref, allq_ref, all_asked_ref, send_sem, recv_sem, own_sem):
    li, sc = lax.axis_index("lists"), lax.axis_index("score")
    mine = (sc // sizes[1], sc % sizes[1], li // sizes[3], li % sizes[3])
    rows = q_ref.shape[0]
    half = rows // 2
    score = sizes[0] * sizes[1]

    def device(at):
        return (at[2] * sizes[3] + at[3], at[0] * sizes[1] + at[1])

    def moved(dim, by):
        return tuple(lax.rem(c + by + n, n) if d == dim else c for d, (c, n) in enumerate(zip(mine, sizes)))

    def block(part, back):
        at = device([lax.rem(c - b + n, n) if b else c for c, b, n in zip(mine, back, sizes)])
        if part == 2:
            return all_asked_ref.at[at[0] * score + at[1]]
        return allq_ref.at[pl.ds(at[1] * rows + part * half, half), at[0]]

    def own(part):
        return asked_ref if part == 2 else q_ref.at[pl.ds(part * half, half)]

    barrier = pltpu.get_barrier_semaphore()
    peers = [(d, by) for d in range(4) for by in range(1, sizes[d])]
    for d, by in peers:
        pl.semaphore_signal(barrier, inc=1, device_id=device(moved(d, by)), device_id_type=MESH)
    pl.semaphore_wait(barrier, len(peers))

    orders = ((0, 1, 2, 3), (0, 2, 1, 3), (0, 1, 2, 3))
    places = list(itertools.product(*(range(n) for n in sizes)))
    number = {back: i for i, back in enumerate(places)}

    def cost(item):
        part, back = item
        return (sum((1 if d == 3 else 3 + b) for d, b in enumerate(back) if b), -part)

    zero = (0, 0, 0, 0)
    sent = []
    own_copies = [pltpu.make_async_copy(own(p), block(p, zero), own_sem.at[p]) for p in range(3)]
    for copy in own_copies:
        copy.start()
    for part, back in sorted(itertools.product(range(3), places), key=cost):
        order = orders[part]
        here = block(part, back)
        last = max([order.index(d) for d in range(4) if back[d]], default=-1)
        if back != zero:
            pltpu.make_async_remote_copy(
                src_ref=here,
                dst_ref=here,
                send_sem=send_sem.at[part, number[back]],
                recv_sem=recv_sem.at[part, number[back]],
                device_id=device(moved(order[last], 1)),
                device_id_type=MESH,
            ).wait_recv()
        for d in order[last + 1 :]:
            for by in range(1, sizes[d]):
                there = number[tuple(by if e == d else b for e, b in enumerate(back))]
                copy = pltpu.make_async_remote_copy(
                    src_ref=own(part) if back == zero else here,
                    dst_ref=here,
                    send_sem=send_sem.at[part, there],
                    recv_sem=recv_sem.at[part, there],
                    device_id=device(moved(d, by)),
                    device_id_type=MESH,
                )
                copy.start()
                sent.append(copy)
    for copy in sent:
        copy.wait_send()
    for copy in own_copies:
        copy.wait()


def spread(queries, asked, lists, score):
    rows, tokens, width = queries.shape
    vmem = pl.BlockSpec(memory_space=pltpu.VMEM)
    devices = lists * score
    return pl.pallas_call(
        functools.partial(spread_kernel, split_sizes(lists, score)),
        out_shape=[
            jax.ShapeDtypeStruct((score * rows, lists, tokens, width), queries.dtype),
            jax.ShapeDtypeStruct((devices,) + asked.shape, asked.dtype),
        ],
        in_specs=[vmem] * 2,
        out_specs=[vmem] * 2,
        scratch_shapes=[
            pltpu.SemaphoreType.DMA((3, devices)),
            pltpu.SemaphoreType.DMA((3, devices)),
            pltpu.SemaphoreType.DMA((3,)),
        ],
        compiler_params=pltpu.CompilerParams(
            collective_id=0, has_side_effects=True, vmem_limit_bytes=16 * 1024 * 1024
        ),
    )(queries, asked)


def before(count):
    spots = jnp.arange(count, dtype=jnp.int32)
    return (spots[:, None] < spots[None, :]).astype(jnp.bfloat16)


def per_device(queries, centroids, codes, scales, centroid_ids, lengths, owners, slots):
    lists, score = lax.axis_size("lists"), lax.axis_size("score")
    devices = lists * score
    me = lax.axis_index("lists") * score + lax.axis_index("score")
    query_rows, per_query = owners.shape[1:]
    capacity = max(4, 2 * -(-query_rows * per_query // devices))
    held = codes.shape[0]

    named_here = (owners[0] * held + slots[0]).reshape(-1, 128)
    allq, asked = spread(queries, named_here, lists, score)
    token_count, width = lists * queries.shape[1], queries.shape[2]
    allq = allq.reshape(score * query_rows, token_count, width)
    asked = asked.reshape(devices, query_rows, per_query)
    mine = lax.dynamic_slice_in_dim(allq, lax.axis_index("score") * query_rows, query_rows, 0)

    inner = lax.dot_general(
        mine.reshape(-1, width), centroids, (((1,), (1,)), ((), ())), preferred_element_type=jnp.float32
    )
    relevance = jnp.max(inner.reshape(query_rows, token_count, -1), axis=1)

    hit = asked // held == me
    named = jnp.any(hit, axis=2)
    slot = jnp.sum(jnp.where(hit, asked % held, 0), axis=2)
    place = jnp.dot(named.astype(jnp.bfloat16), before(query_rows), preferred_element_type=jnp.float32).astype(jnp.int32)
    take = named[:, None, :] & (place[:, None, :] == jnp.arange(capacity, dtype=jnp.int32)[None, :, None])
    group = jnp.arange(devices, dtype=jnp.int32) % score
    query = group[:, None] * query_rows + jnp.arange(query_rows, dtype=jnp.int32)[None, :]
    pickq = jnp.sum(jnp.where(take, query[:, None, :], 0), axis=2).reshape(-1)
    picks = jnp.sum(jnp.where(take, slot[:, None, :], 0), axis=2).reshape(-1)

    done = score_pairs(centroid_ids, lengths, pickq, picks, centroids, codes, scales, allq)
    done = done[:, :PAIRS].reshape(devices, capacity)
    full = jnp.sum(jnp.where(take, done[:, :, None], 0.0), axis=1)
    back = lax.all_to_all(full, AXES, split_axis=0, concat_axis=0, tiled=True)
    which = owners[0][:, :, None] == jnp.arange(devices, dtype=jnp.int32)
    scores = jnp.sum(jnp.where(which, jnp.transpose(back)[:, None, :], 0.0), axis=2)
    return (scores[None], relevance)


def solution(mesh):
    placed = (
        P("score", "lists", None),
        P("lists", None),
        P(("lists", "score"), None, None),
        P(("lists", "score"), None),
        P(("lists", "score"), None),
        P(("lists", "score")),
        P("lists", "score", None),
        P("lists", "score", None),
    )
    return jax.shard_map(
        per_device,
        mesh=mesh,
        in_specs=placed,
        out_specs=(P("lists", "score", None), P("score", "lists")),
        check_vma=False,
    )
```

```python
import functools
import itertools
import math

import jax
import jax.numpy as jnp
from jax import lax
from jax.experimental import pallas as pl
from jax.experimental.pallas import tpu as pltpu
from jax.sharding import PartitionSpec as P

PAIRS = 16
ROWS = 16
AXES = ("lists", "score")


def widen(cent, wide):
    step = 512

    @pl.loop(0, cent.shape[0] // step)
    def _(i):
        rows = pl.ds(pl.multiple_of(i * step, step), step)
        wide[rows, :] = cent[rows, :].astype(jnp.float32)


def rebuild(first_block, blocks, ids_ref, scales_ref, codes, wide, base, vecs_ref):
    held, slot_len, width = codes.shape

    @pl.loop(first_block, first_block + blocks)
    def _(b):
        @pl.loop(0, slot_len // ROWS)
        def _(r):
            first = pl.multiple_of(r * ROWS, ROWS)
            for j in range(ROWS):
                base[pl.ds(first + j, 1), :] = wide[pl.ds(ids_ref[b, first + j], 1), :]

        row = scales_ref[pl.ds(b, 1), :]
        spread = jnp.transpose(jnp.broadcast_to(row, (slot_len, slot_len)))
        if width != slot_len:
            spread = jnp.broadcast_to(spread[:, :1], (slot_len, width))
        vecs_ref[b] = (base[...] + spread * codes[b].astype(jnp.float32)).astype(jnp.bfloat16)


def score_kernel(lens_ref, picks_ref, vecs, q_ref, out_ref):
    held, slot_len, width = vecs.shape
    lanes = lax.broadcasted_iota(jnp.int32, (1, slot_len), 1)

    @pl.loop(0, out_ref.shape[0])
    def _(i):
        acc = jnp.zeros((1, 128), jnp.float32)
        spots = lax.broadcasted_iota(jnp.int32, (1, 128), 1)
        for j in range(PAIRS):
            pick = picks_ref[i * PAIRS + j]
            slot = lax.rem(pick, held)
            inner = lax.dot_general(
                q_ref[lax.div(pick, held)],
                vecs[slot],
                (((1,), (1,)), ((), ())),
                preferred_element_type=jnp.float32,
            )
            inner = jnp.where(lanes < lens_ref[slot], inner, -1e30)
            best = jnp.max(inner, axis=1, keepdims=True)
            total = jnp.sum(best, axis=0, keepdims=True)
            acc = jnp.where(spots == j, total, acc)
        out_ref[pl.ds(i, 1), :] = acc * (1.0 / q_ref.shape[1])


def score_pairs(lens, picks, vecs, allq):
    smem = pl.BlockSpec(memory_space=pltpu.SMEM)
    vmem = pl.BlockSpec(memory_space=pltpu.VMEM)
    return pl.pallas_call(
        score_kernel,
        out_shape=jax.ShapeDtypeStruct((picks.shape[0] // PAIRS, 128), jnp.float32),
        in_specs=[smem] * 2 + [vmem] * 2,
        out_specs=vmem,
        compiler_params=pltpu.CompilerParams(vmem_limit_bytes=24 * 1024 * 1024),
    )(lens, picks, vecs, allq)


MESH = pl.DeviceIdType.MESH


def split_sizes(lists, score):
    core = 2 if lists % 2 == 0 else 1
    inner = 2 if score <= 8 and score % 2 == 0 else math.gcd(score, 4)
    return (score // inner, inner, lists // core, core)


def spread_kernel(
    sizes, q_ref, asked_ref, ids_ref, scales_ref, cent_hbm, codes_hbm, allq_ref, all_asked_ref, vecs_ref,
    cent, codes, wide, base, send_sem, recv_sem, own_sem, load_sem,
):
    loads = [pltpu.make_async_copy(cent_hbm, cent, load_sem.at[0]), pltpu.make_async_copy(codes_hbm, codes, load_sem.at[1])]
    for copy in loads:
        copy.start()
    li, sc = lax.axis_index("lists"), lax.axis_index("score")
    mine = (sc // sizes[1], sc % sizes[1], li // sizes[3], li % sizes[3])
    rows = q_ref.shape[0]
    half = rows // 2
    score = sizes[0] * sizes[1]

    def device(at):
        return (at[2] * sizes[3] + at[3], at[0] * sizes[1] + at[1])

    def moved(dim, by):
        return tuple(lax.rem(c + by + n, n) if d == dim else c for d, (c, n) in enumerate(zip(mine, sizes)))

    def block(part, back):
        at = device([lax.rem(c - b + n, n) if b else c for c, b, n in zip(mine, back, sizes)])
        if part == 2:
            return all_asked_ref.at[at[0] * score + at[1]]
        return allq_ref.at[pl.ds(at[1] * rows + part * half, half), at[0]]

    def own(part):
        return asked_ref if part == 2 else q_ref.at[pl.ds(part * half, half)]

    barrier = pltpu.get_barrier_semaphore()
    peers = [(d, by) for d in range(4) for by in range(1, sizes[d])]
    for d, by in peers:
        pl.semaphore_signal(barrier, inc=1, device_id=device(moved(d, by)), device_id_type=MESH)
    pl.semaphore_wait(barrier, len(peers))

    orders = ((0, 1, 2, 3), (0, 2, 1, 3), (0, 1, 2, 3))
    places = list(itertools.product(*(range(n) for n in sizes)))
    number = {back: i for i, back in enumerate(places)}

    def cost(item):
        part, back = item
        return (sum((1 if d == 3 else 3 + b) for d, b in enumerate(back) if b), -part)

    zero = (0, 0, 0, 0)
    sent = []
    own_copies = [pltpu.make_async_copy(own(p), block(p, zero), own_sem.at[p]) for p in range(3)]
    for copy in own_copies:
        copy.start()
    nodes = sorted(itertools.product(range(3), places), key=cost)
    held = codes.shape[0]
    chunks = math.gcd(held, 8)
    due = {3 + (len(nodes) - 3) * i // chunks: i for i in range(chunks)}
    for turn, (part, back) in enumerate(nodes):
        if turn == 3:
            loads[0].wait()
            widen(cent, wide)
            loads[1].wait()
        if turn in due:
            blocks = held // chunks
            rebuild(due[turn] * blocks, blocks, ids_ref, scales_ref, codes, wide, base, vecs_ref)
        order = orders[part]
        here = block(part, back)
        last = max([order.index(d) for d in range(4) if back[d]], default=-1)
        if back != zero:
            pltpu.make_async_remote_copy(
                src_ref=here,
                dst_ref=here,
                send_sem=send_sem.at[part, number[back]],
                recv_sem=recv_sem.at[part, number[back]],
                device_id=device(moved(order[last], 1)),
                device_id_type=MESH,
            ).wait_recv()
        for d in order[last + 1 :]:
            for by in range(1, sizes[d]):
                there = number[tuple(by if e == d else b for e, b in enumerate(back))]
                copy = pltpu.make_async_remote_copy(
                    src_ref=own(part) if back == zero else here,
                    dst_ref=here,
                    send_sem=send_sem.at[part, there],
                    recv_sem=recv_sem.at[part, there],
                    device_id=device(moved(d, by)),
                    device_id_type=MESH,
                )
                copy.start()
                sent.append(copy)
    for copy in sent:
        copy.wait_send()
    for copy in own_copies:
        copy.wait()


def spread(queries, asked, ids, scales, centroids, codes, lists, score):
    rows, tokens, width = queries.shape
    vmem = pl.BlockSpec(memory_space=pltpu.VMEM)
    smem = pl.BlockSpec(memory_space=pltpu.SMEM)
    hbm = pl.BlockSpec(memory_space=pl.ANY)
    devices = lists * score
    return pl.pallas_call(
        functools.partial(spread_kernel, split_sizes(lists, score)),
        out_shape=[
            jax.ShapeDtypeStruct((score * rows, lists, tokens, width), queries.dtype),
            jax.ShapeDtypeStruct((devices,) + asked.shape, asked.dtype),
            jax.ShapeDtypeStruct(codes.shape, jnp.bfloat16),
        ],
        in_specs=[vmem, vmem, smem, vmem, hbm, hbm],
        out_specs=[vmem] * 3,
        scratch_shapes=[
            pltpu.VMEM(centroids.shape, centroids.dtype),
            pltpu.VMEM(codes.shape, codes.dtype),
            pltpu.VMEM(centroids.shape, jnp.float32),
            pltpu.VMEM(codes.shape[1:], jnp.float32),
            pltpu.SemaphoreType.DMA((3, devices)),
            pltpu.SemaphoreType.DMA((3, devices)),
            pltpu.SemaphoreType.DMA((3,)),
            pltpu.SemaphoreType.DMA((2,)),
        ],
        compiler_params=pltpu.CompilerParams(
            collective_id=0, has_side_effects=True, vmem_limit_bytes=32 * 1024 * 1024
        ),
    )(queries, asked, ids, scales, centroids, codes)


def before(count):
    spots = jnp.arange(count, dtype=jnp.int32)
    return (spots[:, None] < spots[None, :]).astype(jnp.bfloat16)


def per_device(queries, centroids, codes, scales, centroid_ids, lengths, owners, slots):
    lists, score = lax.axis_size("lists"), lax.axis_size("score")
    devices = lists * score
    me = lax.axis_index("lists") * score + lax.axis_index("score")
    query_rows, per_query = owners.shape[1:]
    capacity = max(4, 2 * -(-query_rows * per_query // devices))
    held = codes.shape[0]

    named_here = (owners[0] * held + slots[0]).reshape(-1, 128)
    allq, asked, vecs = spread(
        queries, named_here, centroid_ids, scales, centroids, codes, lists, score
    )
    token_count, width = lists * queries.shape[1], queries.shape[2]
    allq = allq.reshape(score * query_rows, token_count, width)
    asked = asked.reshape(devices, query_rows, per_query)
    mine = lax.dynamic_slice_in_dim(allq, lax.axis_index("score") * query_rows, query_rows, 0)

    inner = lax.dot_general(
        mine.reshape(-1, width), centroids, (((1,), (1,)), ((), ())), preferred_element_type=jnp.float32
    )
    relevance = jnp.max(inner.reshape(query_rows, token_count, -1), axis=1)

    hit = asked // held == me
    named = jnp.any(hit, axis=2)
    slot = jnp.sum(jnp.where(hit, asked % held, 0), axis=2)
    place = jnp.dot(named.astype(jnp.bfloat16), before(query_rows), preferred_element_type=jnp.float32).astype(jnp.int32)
    take = named[:, None, :] & (place[:, None, :] == jnp.arange(capacity, dtype=jnp.int32)[None, :, None])
    group = jnp.arange(devices, dtype=jnp.int32) % score
    query = group[:, None] * query_rows + jnp.arange(query_rows, dtype=jnp.int32)[None, :]
    pick = query * held + slot
    picks = jnp.sum(jnp.where(take, pick[:, None, :], 0), axis=2).reshape(-1)

    done = score_pairs(lengths, picks, vecs, allq)
    done = done[:, :PAIRS].reshape(devices, capacity)
    full = jnp.sum(jnp.where(take, done[:, :, None], 0.0), axis=1)
    back = lax.all_to_all(full, AXES, split_axis=0, concat_axis=0, tiled=True)
    which = owners[0][:, :, None] == jnp.arange(devices, dtype=jnp.int32)
    scores = jnp.sum(jnp.where(which, jnp.transpose(back)[:, None, :], 0.0), axis=2)
    return (scores[None], relevance)


def solution(mesh):
    placed = (
        P("score", "lists", None),
        P("lists", None),
        P(("lists", "score"), None, None),
        P(("lists", "score"), None),
        P(("lists", "score"), None),
        P(("lists", "score")),
        P("lists", "score", None),
        P("lists", "score", None),
    )
    return jax.shard_map(
        per_device,
        mesh=mesh,
        in_specs=placed,
        out_specs=(P("lists", "score", None), P("score", "lists")),
        check_vma=False,
    )
```

```python
import functools
import itertools
import math

import jax
import jax.numpy as jnp
from jax import lax
from jax.experimental import pallas as pl
from jax.experimental.pallas import tpu as pltpu
from jax.sharding import PartitionSpec as P

PAIRS = 64
ROWS = 16
AXES = ("lists", "score")


def widen(cent, wide):
    step = 512

    @pl.loop(0, cent.shape[0] // step)
    def _(i):
        rows = pl.ds(pl.multiple_of(i * step, step), step)
        wide[rows, :] = cent[rows, :].astype(jnp.float32)


def rebuild(first_block, blocks, ids_ref, scales_ref, codes, wide, base, vecs_ref):
    held, slot_len, width = codes.shape

    @pl.loop(first_block, first_block + blocks)
    def _(b):
        @pl.loop(0, slot_len // ROWS)
        def _(r):
            first = pl.multiple_of(r * ROWS, ROWS)
            for j in range(ROWS):
                base[pl.ds(first + j, 1), :] = wide[pl.ds(ids_ref[b, first + j], 1), :]

        row = scales_ref[pl.ds(b, 1), :]
        spread = jnp.transpose(jnp.broadcast_to(row, (slot_len, slot_len)))
        if width != slot_len:
            spread = jnp.broadcast_to(spread[:, :1], (slot_len, width))
        vecs_ref[b] = (base[...] + spread * codes[b].astype(jnp.float32)).astype(jnp.bfloat16)


def score_kernel(lens_ref, picks_ref, vecs, q_ref, out_ref):
    held, slot_len, width = vecs.shape
    lanes = lax.broadcasted_iota(jnp.int32, (1, slot_len), 1)

    @pl.loop(0, out_ref.shape[0])
    def _(i):
        acc = jnp.zeros((1, 128), jnp.float32)
        spots = lax.broadcasted_iota(jnp.int32, (1, 128), 1)
        for j in range(PAIRS):
            pick = picks_ref[i * PAIRS + j]
            slot = lax.rem(pick, held)
            inner = lax.dot_general(
                q_ref[lax.div(pick, held)],
                vecs[slot],
                (((1,), (1,)), ((), ())),
                preferred_element_type=jnp.float32,
            )
            inner = jnp.where(lanes < lens_ref[slot], inner, -1e30)
            best = jnp.max(inner, axis=1, keepdims=True)
            total = jnp.sum(best, axis=0, keepdims=True)
            acc = jnp.where(spots == j, total, acc)
        out_ref[pl.ds(i, 1), :] = acc * (1.0 / q_ref.shape[1])


def score_pairs(lens, picks, vecs, allq):
    smem = pl.BlockSpec(memory_space=pltpu.SMEM)
    vmem = pl.BlockSpec(memory_space=pltpu.VMEM)
    return pl.pallas_call(
        score_kernel,
        out_shape=jax.ShapeDtypeStruct((picks.shape[0] // PAIRS, 128), jnp.float32),
        in_specs=[smem] * 2 + [vmem] * 2,
        out_specs=vmem,
        compiler_params=pltpu.CompilerParams(vmem_limit_bytes=24 * 1024 * 1024),
    )(lens, picks, vecs, allq)


MESH = pl.DeviceIdType.MESH


def split_sizes(lists, score):
    core = 2 if lists % 2 == 0 else 1
    inner = 2 if score <= 8 and score % 2 == 0 else math.gcd(score, 4)
    return (score // inner, inner, lists // core, core)


def spread_kernel(
    sizes, q_ref, asked_ref, ids_hbm, scales_hbm, cent_hbm, codes_hbm, allq_ref, all_asked_ref, vecs_ref,
    ids_ref, scales_ref, cent, codes, wide, base, send_sem, recv_sem, own_sem, load_sem,
):
    pairs = ((cent_hbm, cent), (codes_hbm, codes), (ids_hbm, ids_ref), (scales_hbm, scales_ref))
    loads = [pltpu.make_async_copy(src, dst, load_sem.at[i]) for i, (src, dst) in enumerate(pairs)]
    for copy in loads:
        copy.start()
    li, sc = lax.axis_index("lists"), lax.axis_index("score")
    mine = (sc // sizes[1], sc % sizes[1], li // sizes[3], li % sizes[3])
    rows = q_ref.shape[0]
    half = rows // 2
    score = sizes[0] * sizes[1]

    def device(at):
        return (at[2] * sizes[3] + at[3], at[0] * sizes[1] + at[1])

    def moved(dim, by):
        return tuple(lax.rem(c + by + n, n) if d == dim else c for d, (c, n) in enumerate(zip(mine, sizes)))

    def block(part, back):
        at = device([lax.rem(c - b + n, n) if b else c for c, b, n in zip(mine, back, sizes)])
        if part == 2:
            return all_asked_ref.at[at[0] * score + at[1]]
        return allq_ref.at[pl.ds(at[1] * rows + part * half, half), at[0]]

    def own(part):
        return asked_ref if part == 2 else q_ref.at[pl.ds(part * half, half)]

    barrier = pltpu.get_barrier_semaphore()
    peers = [(d, by) for d in range(4) for by in range(1, sizes[d])]
    for d, by in peers:
        pl.semaphore_signal(barrier, inc=1, device_id=device(moved(d, by)), device_id_type=MESH)
    pl.semaphore_wait(barrier, len(peers))

    orders = ((0, 1, 2, 3), (0, 2, 1, 3), (0, 1, 2, 3))
    places = list(itertools.product(*(range(n) for n in sizes)))
    number = {back: i for i, back in enumerate(places)}

    def cost(item):
        part, back = item
        return (sum((1 if d == 3 else 3 + b) for d, b in enumerate(back) if b), -part)

    zero = (0, 0, 0, 0)
    sent = []
    own_copies = [pltpu.make_async_copy(own(p), block(p, zero), own_sem.at[p]) for p in range(3)]
    for copy in own_copies:
        copy.start()
    nodes = sorted(itertools.product(range(3), places), key=cost)
    held = codes.shape[0]
    chunks = math.gcd(held, 8)
    due = {3 + (len(nodes) - 3) * i // chunks: i for i in range(chunks)}
    for turn, (part, back) in enumerate(nodes):
        if turn == 3:
            loads[0].wait()
            widen(cent, wide)
            for copy in loads[1:]:
                copy.wait()
        if turn in due:
            blocks = held // chunks
            rebuild(due[turn] * blocks, blocks, ids_ref, scales_ref, codes, wide, base, vecs_ref)
        order = orders[part]
        here = block(part, back)
        last = max([order.index(d) for d in range(4) if back[d]], default=-1)
        if back != zero:
            pltpu.make_async_remote_copy(
                src_ref=here,
                dst_ref=here,
                send_sem=send_sem.at[part, number[back]],
                recv_sem=recv_sem.at[part, number[back]],
                device_id=device(moved(order[last], 1)),
                device_id_type=MESH,
            ).wait_recv()
        for d in order[last + 1 :]:
            for by in range(1, sizes[d]):
                there = number[tuple(by if e == d else b for e, b in enumerate(back))]
                copy = pltpu.make_async_remote_copy(
                    src_ref=own(part) if back == zero else here,
                    dst_ref=here,
                    send_sem=send_sem.at[part, there],
                    recv_sem=recv_sem.at[part, there],
                    device_id=device(moved(d, by)),
                    device_id_type=MESH,
                )
                copy.start()
                sent.append(copy)
    for copy in sent:
        copy.wait_send()
    for copy in own_copies:
        copy.wait()


def spread(queries, asked, ids, scales, centroids, codes, lists, score):
    rows, tokens, width = queries.shape
    vmem = pl.BlockSpec(memory_space=pltpu.VMEM)
    hbm = pl.BlockSpec(memory_space=pltpu.MemorySpace.HBM)
    devices = lists * score
    return pl.pallas_call(
        functools.partial(spread_kernel, split_sizes(lists, score)),
        out_shape=[
            jax.ShapeDtypeStruct((score * rows, lists, tokens, width), queries.dtype),
            jax.ShapeDtypeStruct((devices,) + asked.shape, asked.dtype),
            jax.ShapeDtypeStruct(codes.shape, jnp.bfloat16),
        ],
        in_specs=[hbm, vmem, hbm, hbm, hbm, hbm],
        out_specs=[vmem] * 3,
        scratch_shapes=[
            pltpu.SMEM(ids.shape, ids.dtype),
            pltpu.VMEM(scales.shape, scales.dtype),
            pltpu.VMEM(centroids.shape, centroids.dtype),
            pltpu.VMEM(codes.shape, codes.dtype),
            pltpu.VMEM(centroids.shape, jnp.float32),
            pltpu.VMEM(codes.shape[1:], jnp.float32),
            pltpu.SemaphoreType.DMA((3, devices)),
            pltpu.SemaphoreType.DMA((3, devices)),
            pltpu.SemaphoreType.DMA((3,)),
            pltpu.SemaphoreType.DMA((4,)),
        ],
        compiler_params=pltpu.CompilerParams(
            collective_id=0, has_side_effects=True, vmem_limit_bytes=58 * 1024 * 1024
        ),
    )(queries, asked, ids, scales, centroids, codes)


def before(count):
    spots = jnp.arange(count, dtype=jnp.int32)
    return (spots[:, None] < spots[None, :]).astype(jnp.bfloat16)


def per_device(queries, centroids, codes, scales, centroid_ids, lengths, owners, slots):
    lists, score = lax.axis_size("lists"), lax.axis_size("score")
    devices = lists * score
    me = lax.axis_index("lists") * score + lax.axis_index("score")
    query_rows, per_query = owners.shape[1:]
    capacity = max(4, 2 * -(-query_rows * per_query // devices))
    held = codes.shape[0]

    named_here = (owners[0] * held + slots[0]).reshape(-1, 128)
    allq, asked, vecs = spread(
        queries, named_here, centroid_ids, scales, centroids, codes, lists, score
    )
    token_count, width = lists * queries.shape[1], queries.shape[2]
    allq = allq.reshape(score * query_rows, token_count, width)
    asked = asked.reshape(devices, query_rows, per_query)
    mine = lax.dynamic_slice_in_dim(allq, lax.axis_index("score") * query_rows, query_rows, 0)

    inner = lax.dot_general(
        mine.reshape(-1, width), centroids, (((1,), (1,)), ((), ())), preferred_element_type=jnp.float32
    )
    relevance = jnp.max(inner.reshape(query_rows, token_count, -1), axis=1)

    hit = asked // held == me
    named = jnp.any(hit, axis=2)
    slot = jnp.sum(jnp.where(hit, asked % held, 0), axis=2)
    place = jnp.dot(named.astype(jnp.bfloat16), before(query_rows), preferred_element_type=jnp.float32).astype(jnp.int32)
    take = named[:, None, :] & (place[:, None, :] == jnp.arange(capacity, dtype=jnp.int32)[None, :, None])
    group = jnp.arange(devices, dtype=jnp.int32) % score
    query = group[:, None] * query_rows + jnp.arange(query_rows, dtype=jnp.int32)[None, :]
    pick = query * held + slot
    picks = jnp.sum(jnp.where(take, pick[:, None, :], 0), axis=2).reshape(-1)

    done = score_pairs(lengths, picks, vecs, allq)
    done = done[:, :PAIRS].reshape(devices, capacity)
    full = jnp.sum(jnp.where(take, done[:, :, None], 0.0), axis=1)
    back = lax.all_to_all(full, AXES, split_axis=0, concat_axis=0, tiled=True)
    which = owners[0][:, :, None] == jnp.arange(devices, dtype=jnp.int32)
    scores = jnp.sum(jnp.where(which, jnp.transpose(back)[:, None, :], 0.0), axis=2)
    return (scores[None], relevance)


def solution(mesh):
    placed = (
        P("score", "lists", None),
        P("lists", None),
        P(("lists", "score"), None, None),
        P(("lists", "score"), None),
        P(("lists", "score"), None),
        P(("lists", "score")),
        P("lists", "score", None),
        P("lists", "score", None),
    )
    return jax.shard_map(
        per_device,
        mesh=mesh,
        in_specs=placed,
        out_specs=(P("lists", "score", None), P("score", "lists")),
        check_vma=False,
    )
```
